32 devices in a mesh: ctx: 16 (over z, y, core), sec: 2 (over x).
Axes of the slice: x: 2, y: 2, z: 4, core: 2. Of those that a mesh axis runs over, the one named last changes fastest.
Arguments:
- query_nope: bfloat16 [1024, 8192], P('ctx', 'sec'), may hold values from -6 to 6
- query_rope: bfloat16 [1024, 4096], P('ctx', 'sec'), may hold values from -8 to 8
- key_latent: bfloat16 [1024, 512], P('ctx'), may hold values from -6 to 6
- key_rope: bfloat16 [1024, 64], P('ctx'), may hold values from -8 to 8
- key_up: bfloat16 [64, 512, 128], P('sec'), may hold values from -0.25 to 0.25
- value_up: bfloat16 [64, 512, 128], P('sec'), may hold values from -1 to 1
- routed_tokens: bfloat16 [4096, 7168], P(('ctx', 'sec')), may hold values from -6 to 6
- expert_ids: int32 [4096, 8], P(('ctx', 'sec')), may hold values from 0 to 255, as said below
- expert_gates: float32 [4096, 8], P(('ctx', 'sec')), may hold values from 0.2 to 2
- gate_weight: bfloat16 [7168, 8192], P(None, ('ctx', 'sec')), may hold values from -0.0625 to 0.0625
- up_weight: bfloat16 [7168, 8192], P(None, ('ctx', 'sec')), may hold values from -0.0625 to 0.0625
- down_weight: bfloat16 [8192, 7168], P(('ctx', 'sec')), may hold values from -0.125 to 0.125
Outputs:
- attention_out: bfloat16 [1024, 8192], P('ctx', 'sec')
- routed_out: bfloat16 [4096, 7168], P(('ctx', 'sec'))
The draws below stay inside these ranges and needn't reach their ends.
Inputs may be any that keep to these rules, and one draw needn't show every extreme that they name: `expert_ids`: each row names 8 different experts, at most one of them below 4. Within each aligned block of 128 rows (the rows of one device) no expert below 4 is named more than 4 times, and in every draw one expert below 4 is named exactly 4 times in every block.
All inputs are finite; a program needn't handle non-finite values.
Results may differ from the reference program's by a relative error of at most 0.008.
Values may be sent and summed in bfloat16 or wider, within the bound.
A program may use at most 192 MiB of HBM per device.

```python
import jax
import jax.numpy as jnp
from jax import lax

D = 7168
FF = 2048
EXPERTS = 256
TOPK = 8
LAT = 512
ROPE = 64
NOPE = 128
VDIM = 128
HEADS = 64
CAP = 4
MTOK_DEV = 128
EXP_ROUND = 4
SEQ = 1024
MTOKENS = 4096
ROUND_FF = 8192
N_CTX = 16
N_SEC = 2


def draw_query_rope(key, part):
    array_shape = (SEQ, HEADS * ROPE)
    values = jnp.clip(jax.random.normal(jax.random.fold_in(key, 1), array_shape, jnp.float32), -6.0, 6.0)
    return values.astype(jnp.bfloat16)


def draw_key_rope(key, part):
    array_shape = (SEQ, ROPE)
    values = jnp.clip(jax.random.normal(jax.random.fold_in(key, 2), array_shape, jnp.float32), -6.0, 6.0)
    return values.astype(jnp.bfloat16)


def draw_expert_ids(key, part):
    block_count = MTOKENS // MTOK_DEV
    outside_count = EXPERTS - EXP_ROUND
    scores = jax.random.randint(jax.random.fold_in(key, 1), (MTOKENS, outside_count), 0, 1 << 20)
    scores = scores * outside_count + jnp.arange(outside_count, dtype=jnp.int32)[None, :]
    picked = lax.top_k(scores, TOPK)[1].astype(jnp.int32) + EXP_ROUND
    levels = jax.random.randint(jax.random.fold_in(key, 2), (EXP_ROUND,), 1, 5)
    hot_expert = jax.random.randint(jax.random.fold_in(key, 3), (), 0, EXP_ROUND)
    counts = jax.random.randint(jax.random.fold_in(key, 4), (block_count, EXP_ROUND), 0, levels * CAP // 4 + 1)
    expert_range = jnp.arange(EXP_ROUND, dtype=jnp.int32)
    counts = jnp.where(expert_range[None, :] == hot_expert, CAP, counts)
    starts = jnp.cumsum(counts, axis=1) - counts
    block_keys = jax.random.split(jax.random.fold_in(key, 5), block_count)
    rank_rows = jax.vmap(lambda block_key: jax.random.permutation(block_key, MTOK_DEV))(block_keys)
    inside = (rank_rows[:, :, None] >= starts[:, None, :]) & (rank_rows[:, :, None] < (starts + counts)[:, None, :])
    member = jnp.any(inside, axis=2).reshape(MTOKENS)
    chosen = jnp.sum(jnp.where(inside, expert_range[None, None, :], 0), axis=2).reshape(MTOKENS)
    column = jax.random.randint(jax.random.fold_in(key, 6), (MTOKENS,), 0, TOPK)
    replace = member[:, None] & (jnp.arange(TOPK, dtype=jnp.int32)[None, :] == column[:, None])
    return jnp.where(replace, chosen[:, None], picked).astype(jnp.int32)


def steps_of(key, extent, shards, smallest, top_value):
    def one(dim, parts):
        heights = jax.random.uniform(jax.random.fold_in(jax.random.fold_in(key, 6), dim), (parts,), jnp.float32, smallest / len(shards), top_value / len(shards))
        return jnp.repeat(jnp.exp(heights), extent[dim] // parts).reshape((-1,) + (1,) * (len(extent) - dim - 1))

    gain = one(*shards[0])
    for cut in shards[1:]:
        gain = gain * one(*cut)
    return gain


def normal_values(rng, extent, width, limit, pieces=(), kind=jnp.bfloat16):
    array = jax.random.normal(rng, extent, jnp.float32) * width
    if len(pieces) > 0:
        array = steps_of(rng, extent, pieces, -0.22, 0.18) * array
    return jnp.clip(array, min=-limit, max=limit).astype(kind)


def setup_inputs(seed: int = 0) -> dict:
    streams_of = jax.random.split(jax.random.key(seed), 13)
    return {
        "query_nope": normal_values(streams_of[0], (SEQ, HEADS * NOPE), 1.0, 6.0, ((0, 16), (1, 2))),
        "query_rope": draw_query_rope(jax.random.fold_in(streams_of[12], 71), 0),
        "key_latent": normal_values(streams_of[2], (SEQ, LAT), 1.0, 6.0, ((0, 16),)),
        "key_rope": draw_key_rope(jax.random.fold_in(streams_of[12], 71), 0),
        "key_up": normal_values(streams_of[4], (HEADS, LAT, NOPE), LAT ** -0.5, 0.25, ((0, 2),)),
        "value_up": normal_values(streams_of[5], (HEADS, LAT, VDIM), (LAT // 16) ** -0.5, 1.0, ((0, 2),)),
        "routed_tokens": normal_values(streams_of[6], (MTOKENS, D), 1.0, 6.0, ((0, 32),)),
        "expert_ids": draw_expert_ids(jax.random.fold_in(streams_of[12], 71), 0),
        "expert_gates": jnp.clip(0.2 + 1.8 * jax.random.uniform(streams_of[8], (MTOKENS, TOPK), jnp.float32) ** steps_of(streams_of[8], (MTOKENS, TOPK), ((0, 32),), -0.2, 0.2), 0.2, 2.0),
        "gate_weight": normal_values(streams_of[9], (D, ROUND_FF), D ** -0.5, 0.0625, ((1, 32),)),
        "up_weight": normal_values(streams_of[10], (D, ROUND_FF), D ** -0.5, 0.0625, ((1, 32),)),
        "down_weight": normal_values(streams_of[11], (ROUND_FF, D), FF ** -0.5, 0.125, ((0, 32),)),
    }


def head_attention(query_latent, query_rotary, key_latent, key_rope, value_map):
    score_scale = (NOPE + ROPE) ** -0.5
    scores = jnp.dot(query_latent, key_latent.T, preferred_element_type=jnp.float32)
    scores = (scores + jnp.dot(query_rotary, key_rope.T, preferred_element_type=jnp.float32)) * score_scale
    places = jnp.arange(SEQ, dtype=jnp.int32)
    allowed = places[None, :] <= places[:, None]
    scores = jnp.where(allowed, scores, -jnp.inf)
    row_max = jnp.max(scores, axis=1, keepdims=True)
    exponent = jnp.where(allowed, jnp.exp(scores - row_max), 0.0)
    row_sum = jnp.sum(exponent, axis=1, keepdims=True)
    weights = exponent.astype(jnp.bfloat16)
    latent_out = (jnp.dot(weights, key_latent, preferred_element_type=jnp.float32) / row_sum).astype(jnp.bfloat16)
    return jnp.dot(latent_out, value_map, preferred_element_type=jnp.float32).astype(jnp.bfloat16)


def attention(query_nope, query_rope, key_latent, key_rope, key_up, value_up):
    nope_heads = query_nope.reshape(SEQ, HEADS, NOPE)
    rope_heads = query_rope.reshape(SEQ, HEADS, ROPE)

    def one_head(head_index):
        query_latent = jnp.dot(nope_heads[:, head_index, :], key_up[head_index].T, preferred_element_type=jnp.float32).astype(jnp.bfloat16)
        return head_attention(query_latent, rope_heads[:, head_index, :], key_latent, key_rope, value_up[head_index])

    per_head = lax.map(one_head, jnp.arange(HEADS, dtype=jnp.int32))
    return jnp.transpose(per_head, (1, 0, 2)).reshape(SEQ, HEADS * VDIM)


def routed_experts(routed_tokens, expert_ids, expert_gates, gate_weight, up_weight, down_weight):
    budget_rows = N_CTX * N_SEC * CAP
    slot_places = jnp.arange(budget_rows, dtype=jnp.int32)

    def one_expert(summed, expert):
        chosen = expert_ids == expert
        is_named = jnp.any(chosen, axis=1)
        coefficient = jnp.sum(jnp.where(chosen, expert_gates, 0.0), axis=1)
        named_count = jnp.sum(is_named.astype(jnp.int32))
        token_index = jnp.nonzero(is_named, size=budget_rows, fill_value=0)[0].astype(jnp.int32)
        picked_rows = routed_tokens[token_index]
        column_start = expert * FF
        gate_cols = lax.dynamic_slice_in_dim(gate_weight, column_start, FF, 1)
        up_cols = lax.dynamic_slice_in_dim(up_weight, column_start, FF, 1)
        down_rows = lax.dynamic_slice_in_dim(down_weight, column_start, FF, 0)
        gate_act = jnp.dot(picked_rows, gate_cols, preferred_element_type=jnp.float32)
        up_act = jnp.dot(picked_rows, up_cols, preferred_element_type=jnp.float32)
        hidden = (jax.nn.silu(gate_act) * up_act).astype(jnp.bfloat16)
        expert_out = jnp.dot(hidden, down_rows, preferred_element_type=jnp.float32)
        row_scale = jnp.where(slot_places < named_count, coefficient[token_index], 0.0)
        return summed.at[token_index].add(row_scale[:, None] * expert_out), None

    start_sum = jnp.zeros((MTOKENS, D), jnp.float32)
    summed, _ = lax.scan(one_expert, start_sum, jnp.arange(EXP_ROUND, dtype=jnp.int32))
    return summed.astype(jnp.bfloat16)


def reference(query_nope, query_rope, key_latent, key_rope, key_up, value_up, routed_tokens, expert_ids, expert_gates, gate_weight, up_weight, down_weight):
    attention_out = attention(query_nope, query_rope, key_latent, key_rope, key_up, value_up)
    routed_out = routed_experts(routed_tokens, expert_ids, expert_gates, gate_weight, up_weight, down_weight)
    return (attention_out, routed_out)
```

```python
import functools

import jax
import jax.numpy as jnp
from jax import lax
from jax.experimental import pallas as pl
from jax.experimental.pallas import tpu as pltpu
from jax.sharding import PartitionSpec as P

CAP = 4
SPLIT = 8
CHUNKS = 4
MESH_ID = pl.DeviceIdType.MESH
F32 = jnp.float32
BF16 = jnp.bfloat16
NT = (((1,), (1,)), ((), ()))


def kernel(
    dims,
    ids_ref,
    gates_ref,
    klat_ref,
    krope_ref,
    tok_hbm,
    qn_hbm,
    qr_hbm,
    ku_hbm,
    vu_hbm,
    gw_hbm,
    uw_hbm,
    dw_hbm,
    att_ref,
    rout_ref,
    tok,
    qn,
    qr,
    ku,
    vu,
    gw,
    uw,
    dw,
    qcat,
    keys,
    kown,
    outg,
    zbuf,
    arr,
    part,
    r1,
    s1,
    r2,
    s2,
    r3,
    rbuf,
    resb,
    wmix,
    load_sem,
    ksend,
    krecv,
    zsend,
    zrecv,
    asend,
    arecv,
    rsend,
    rrecv,
    bsend,
    brecv,
):
    groups, n_sec, rows, heads, lat, ropew, nope, hb = dims
    slots = groups * CAP
    width = tok.shape[1]
    cw = width // CHUNKS
    half = width // 2
    tokens = tok.shape[0]
    ctx = lax.axis_index("ctx")
    sec = lax.axis_index("sec")
    me = ctx * n_sec + sec
    g = me // SPLIT
    m = lax.rem(me, SPLIT)
    bx = lax.rem(m, 2)
    bc = lax.rem(m // 2, 2)
    by = m // 4
    mx = m + 1 - 2 * bx
    mc = m + 2 - 4 * bc
    my = m + 4 - 8 * by

    def dev(group, member):
        index = group * SPLIT + member
        return (index // n_sec, lax.rem(index, n_sec))

    def rcopy(src, dst, ss, rs, target):
        return pltpu.make_async_remote_copy(
            src_ref=src, dst_ref=dst, send_sem=ss, recv_sem=rs,
            device_id=target, device_id_type=MESH_ID,
        )

    nx, nc, ny = dev(g, mx), dev(g, mc), dev(g, my)
    others = [lax.rem(g + step, groups) for step in range(1, groups)]

    barrier = pltpu.get_barrier_semaphore()
    for target in [nx, nc, ny] + [dev(o, m) for o in others]:
        pl.semaphore_signal(barrier, inc=1, device_id=target, device_id_type=MESH_ID)

    pairs = [
        (tok_hbm, tok), (qn_hbm, qn), (qr_hbm, qr), (ku_hbm, ku),
        (gw_hbm, gw), (uw_hbm, uw), (dw_hbm, dw), (vu_hbm, vu),
    ]
    loads = [pltpu.make_async_copy(a, b, load_sem.at[i]) for i, (a, b) in enumerate(pairs)]
    for load in loads:
        load.start()

    lanes = wmix.shape[1]
    lane = lax.broadcasted_iota(jnp.int32, (tokens, lanes), 1)
    slot = lane & (slots - 1)
    expert = slot // CAP
    matches = jnp.zeros((tokens, lanes), F32)
    gate = jnp.zeros((tokens, lanes), F32)
    for k in range(ids_ref.shape[1]):
        hit = ids_ref[:, k : k + 1] == expert
        matches = jnp.where(hit, 1.0, matches)
        gate = gate + jnp.where(hit, gates_ref[:, k : k + 1], 0.0)
    earlier = (
        lax.broadcasted_iota(jnp.int32, (tokens, tokens), 1)
        < lax.broadcasted_iota(jnp.int32, (tokens, tokens), 0)
    )
    rank = jnp.dot(
        jnp.where(earlier, 1.0, 0.0).astype(BF16), matches.astype(BF16), preferred_element_type=F32
    )
    chosen = jnp.where(rank == (slot & (CAP - 1)).astype(F32), matches, 0.0)
    weight = chosen * gate
    w1 = weight.astype(BF16).astype(F32)
    w2 = (weight - w1).astype(BF16).astype(F32)
    w3 = weight - w1 - w2
    wmix[...] = jnp.where(
        lane < slots, w1, jnp.where(lane < 2 * slots, w2, jnp.where(lane < 3 * slots, w3, 0.0))
    ).astype(BF16)
    picker = chosen[:, :128].T[:slots].astype(BF16)

    kown[:, :lat] = klat_ref[...]
    kown[:, lat:] = jnp.concatenate([krope_ref[...], krope_ref[...]], axis=1)

    loads[0].wait()

    @pl.loop(0, CHUNKS)
    def _(c):
        cols = pl.ds(pl.multiple_of(c * cw, cw), cw)
        picked = jnp.dot(picker, tok[:, cols], preferred_element_type=F32)
        for e in range(groups):
            outg[e, :, cols] = picked[e * CAP : (e + 1) * CAP].astype(BF16)

    pl.semaphore_wait(barrier, 3 + len(others))

    zc = []
    for i, o in enumerate(others):
        cp = rcopy(outg.at[o], zbuf.at[g], zsend.at[i], zrecv.at[g], dev(o, m))
        cp.start()
        zc.append(cp)
    kc = []
    for i, o in enumerate(others):
        cp = rcopy(kown, keys.at[ctx], ksend.at[i], krecv.at[ctx], dev(o, m))
        cp.start()
        kc.append(cp)
    zbuf[g] = outg[g]
    keys[ctx] = kown[...]

    loads[1].wait()
    loads[2].wait()
    loads[3].wait()

    @pl.loop(0, heads // 2)
    def _(p):
        rope = qr[:, pl.ds(pl.multiple_of(p * 2 * ropew, 2 * ropew), 2 * ropew)]
        low = lax.broadcasted_iota(jnp.int32, rope.shape, 1) < ropew
        for k in range(2):
            h = p * 2 + k
            q = qn[:, pl.ds(pl.multiple_of(h * nope, nope), nope)]
            latent = lax.dot_general(q, ku[h], NT, preferred_element_type=F32)
            place = pl.ds(pl.multiple_of(h * rows, rows), rows)
            qcat[place, :lat] = latent.astype(BF16)
            keep = low if k == 0 else jnp.logical_not(low)
            qcat[place, lat:] = jnp.where(keep, rope.astype(F32), 0.0).astype(BF16)

    def zwait(i, o):
        rcopy(outg.at[o], zbuf.at[o], zsend.at[i], zrecv.at[o], dev(o, m)).wait_recv()

    for i, o in enumerate(others):
        zwait(i, o)

    @pl.loop(0, CHUNKS)
    def _(c):
        cols = pl.ds(pl.multiple_of(c * cw, cw), cw)
        blocks = [zbuf[e, :, cols].astype(F32) for e in range(groups)]
        arr[m, :, cols] = jnp.concatenate(blocks, axis=0).astype(BF16)

    left, right = pl.ds(0, half), pl.ds(half, half)
    halves = (left, right)
    pending = []

    def spread(kind, member, h, target):
        piece = arr.at[member, :, halves[h]]
        cp = rcopy(piece, piece, asend.at[kind, h], arecv.at[member, h], target)
        cp.start()
        pending.append(cp)

    def arrive(member, h):
        piece = arr.at[member, :, halves[h]]
        rcopy(piece, piece, asend.at[0, h], arecv.at[member, h], nx).wait_recv()

    mxy = mx + my - m
    spread(0, m, 0, nx)
    spread(1, m, 1, ny)
    spread(0, m, 1, nx)
    spread(1, m, 0, ny)
    spread(2, m, 0, nc)
    spread(2, m, 1, nc)

    def kshard(group, member):
        return (group * SPLIT + member) // n_sec

    def kpass(kind, group, member, target):
        piece = keys.at[kshard(group, member)]
        cp = rcopy(piece, piece, ksend.at[len(others) + kind * groups + group],
                   krecv.at[kshard(group, member)], target)
        cp.start()
        pending.append(cp)

    def karrive(group, member):
        piece = keys.at[kshard(group, member)]
        rcopy(piece, piece, ksend.at[0], krecv.at[kshard(group, member)], nx).wait_recv()

    arrive(mx, 0)
    spread(3, mx, 0, ny)
    arrive(my, 1)
    spread(3, my, 1, nx)
    spread(4, mx, 0, nc)
    spread(5, my, 1, nc)
    arrive(mx, 1)
    spread(4, mx, 1, nc)
    arrive(my, 0)
    spread(5, my, 0, nc)
    kpass(0, g, m, ny)
    kpass(1, g, m, nc)
    for o in others:
        karrive(o, m)
        kpass(0, o, m, ny)
        kpass(1, o, m, nc)
    arrive(mxy, 0)
    spread(6, mxy, 0, nc)
    arrive(mxy, 1)
    spread(6, mxy, 1, nc)
    for o in [g] + others:
        karrive(o, my)
        kpass(2, o, my, nc)
    mcx, mcy = mx + mc - m, my + mc - m
    for member in (mc, mcx, mcy, mxy + mc - m):
        arrive(member, 0)
        arrive(member, 1)
    loads[4].wait()
    loads[5].wait()
    loads[6].wait()

    count = SPLIT * slots
    step_w = 512
    ff = gw.shape[1]

    def gate_up(k, acc):
        cols = pl.ds(pl.multiple_of(k * step_w, step_w), step_w)
        x = arr[:, :, cols].reshape(count, step_w)
        return (
            acc[0] + jnp.dot(x, gw[cols], preferred_element_type=F32),
            acc[1] + jnp.dot(x, uw[cols], preferred_element_type=F32),
        )

    zero = jnp.zeros((count, ff), F32)
    gate_act, up_act = lax.fori_loop(0, width // step_w, gate_up, (zero, zero))
    hidden = (gate_act / (1.0 + jnp.exp(-gate_act)) * up_act).astype(BF16)

    c1, c2, c3 = [], [], []
    for c in range(CHUNKS):
        value = jnp.dot(hidden, dw[:, c * cw : (c + 1) * cw], preferred_element_type=F32)
        part[c] = value.astype(BF16).reshape(2, 2, 2, slots, cw)
        cp = rcopy(part.at[c, :, 1 - bc], r1.at[c], rsend.at[0, c], rrecv.at[0, c], nc)
        cp.start()
        c1.append(cp)

    loads[7].wait()
    for o in [g] + others:
        karrive(o, mc)
        karrive(o, mcy)

    seq = keys.shape[0] * keys.shape[1]
    block = hb * rows
    scale = (nope + ropew) ** -0.5

    def attend(first, last):
        @pl.loop(first, last)
        def _(b):
            q = qcat[pl.ds(pl.multiple_of(b * block, block), block)]
            kk = keys[...].reshape(seq, keys.shape[2])
            score = lax.dot_general(q, kk, NT, preferred_element_type=F32) * scale
            place = ctx * rows + (
                lax.broadcasted_iota(jnp.int32, (block, seq), 0) & (rows - 1)
            )
            allowed = lax.broadcasted_iota(jnp.int32, (block, seq), 1) <= place
            score = jnp.where(allowed, score, -1e30)
            top = jnp.max(score, axis=1, keepdims=True)
            expo = jnp.exp(score - top)
            total = jnp.sum(expo, axis=1, keepdims=True)
            mixed = jnp.dot(expo.astype(BF16), kk[:, :lat], preferred_element_type=F32)
            mixed = (mixed / total).astype(BF16)
            for k in range(hb):
                h = b * hb + k
                value = jnp.dot(
                    mixed[k * rows : (k + 1) * rows], vu[h], preferred_element_type=F32
                )
                vdim = value.shape[1]
                att_ref[:, pl.ds(pl.multiple_of(h * vdim, vdim), vdim)] = value.astype(BF16)

    nb = heads // hb
    attend(0, nb // 4)

    for c in range(CHUNKS):
        c1[c].wait_recv()
        for a in range(2):
            for b in range(2):
                s1[c, a, b] = (part[c, a, bc, b].astype(F32) + r1[c, a, b].astype(F32)).astype(BF16)
        src = s1.at[c, :, 1 - bx] if c % 2 == 0 else s1.at[c, 1 - by]
        cp = rcopy(src, r2.at[c], rsend.at[1, c], rrecv.at[1, c], nx if c % 2 == 0 else ny)
        cp.start()
        c2.append(cp)

    attend(nb // 4, nb // 2)

    for c in range(CHUNKS):
        c2[c].wait_recv()
        for a in range(2):
            mine = s1[c, a, bx] if c % 2 == 0 else s1[c, by, a]
            s2[c, a] = (mine.astype(F32) + r2[c, a].astype(F32)).astype(BF16)
        keep = by if c % 2 == 0 else bx
        cp = rcopy(s2.at[c, 1 - keep], r3.at[c], rsend.at[2, c], rrecv.at[2, c],
                   ny if c % 2 == 0 else nx)
        cp.start()
        c3.append(cp)

    attend(nb // 2, nb // 2 + nb // 4)

    for c in range(CHUNKS):
        c3[c].wait_recv()
        keep = by if c % 2 == 0 else bx
        total = s2[c, keep].astype(F32) + r3[c].astype(F32)
        for e in range(groups):
            rbuf[e, :, c * cw : (c + 1) * cw] = total[e * CAP : (e + 1) * CAP].astype(BF16)

    bc_list = []
    for i, o in enumerate(others):
        cp = rcopy(rbuf.at[o], resb.at[g], bsend.at[i], brecv.at[g], dev(o, m))
        cp.start()
        bc_list.append(cp)
    resb[g] = rbuf[g]

    attend(nb // 2 + nb // 4, nb)

    for i, o in enumerate(others):
        rcopy(rbuf.at[o], resb.at[o], bsend.at[i], brecv.at[o], dev(o, m)).wait_recv()

    @pl.loop(0, CHUNKS)
    def _(c):
        cols = pl.ds(pl.multiple_of(c * cw, cw), cw)
        blocks = [resb[e, :, cols].astype(F32) for e in range(groups)]
        block_rows = jnp.concatenate(blocks, axis=0)
        tall = jnp.concatenate([block_rows] * (lanes // slots), axis=0).astype(BF16)
        rout_ref[:, cols] = jnp.dot(wmix[...], tall, preferred_element_type=F32).astype(BF16)

    for cp in zc + kc + pending + c1 + c2 + c3 + bc_list:
        cp.wait_send()


def local(n_ctx, n_sec, qn, qr, klat, krope, ku, vu, tok, ids, gates, gw, uw, dw):
    devices = n_ctx * n_sec
    groups = devices // SPLIT
    slots = groups * CAP
    rows = qn.shape[0]
    heads, lat, nope = ku.shape
    ropew = krope.shape[1]
    width = tok.shape[1]
    cw = width // CHUNKS
    kw = lat + 2 * ropew
    hb = 4 if n_ctx * rows <= 2048 else 1
    hb = min(hb, heads)
    lanes = -(-3 * slots // 128) * 128
    dims = (groups, n_sec, rows, heads, lat, ropew, nope, hb)
    v = pl.BlockSpec(memory_space=pltpu.VMEM)
    a = pl.BlockSpec(memory_space=pl.ANY)
    dma = pltpu.SemaphoreType.DMA
    att, rout = pl.pallas_call(
        functools.partial(kernel, dims),
        out_shape=(
            jax.ShapeDtypeStruct((rows, heads * vu.shape[2]), BF16),
            jax.ShapeDtypeStruct(tok.shape, BF16),
        ),
        in_specs=[v, v, v, v] + [a] * 8,
        out_specs=(v, v),
        scratch_shapes=[
            pltpu.VMEM(tok.shape, BF16),
            pltpu.VMEM(qn.shape, BF16),
            pltpu.VMEM(qr.shape, BF16),
            pltpu.VMEM(ku.shape, BF16),
            pltpu.VMEM(vu.shape, BF16),
            pltpu.VMEM(gw.shape, BF16),
            pltpu.VMEM(uw.shape, BF16),
            pltpu.VMEM(dw.shape, BF16),
            pltpu.VMEM((heads * rows, kw), BF16),
            pltpu.VMEM((n_ctx, rows, kw), BF16),
            pltpu.VMEM((rows, kw), BF16),
            pltpu.VMEM((groups, CAP, width), BF16),
            pltpu.VMEM((groups, CAP, width), BF16),
            pltpu.VMEM((SPLIT, slots, width), BF16),
            pltpu.VMEM((CHUNKS, 2, 2, 2, slots, cw), BF16),
            pltpu.VMEM((CHUNKS, 2, 2, slots, cw), BF16),
            pltpu.VMEM((CHUNKS, 2, 2, slots, cw), BF16),
            pltpu.VMEM((CHUNKS, 2, slots, cw), BF16),
            pltpu.VMEM((CHUNKS, 2, slots, cw), BF16),
            pltpu.VMEM((CHUNKS, slots, cw), BF16),
            pltpu.VMEM((groups, CAP, width), BF16),
            pltpu.VMEM((groups, CAP, width), BF16),
            pltpu.VMEM((tok.shape[0], lanes), BF16),
            dma((8,)),
            dma((groups - 1 + 3 * groups,)),
            dma((n_ctx,)),
            dma((groups,)),
            dma((groups,)),
            dma((7, 2)),
            dma((SPLIT, 2)),
            dma((3, CHUNKS)),
            dma((3, CHUNKS)),
            dma((groups,)),
            dma((groups,)),
        ],
        compiler_params=pltpu.CompilerParams(
            collective_id=0, has_side_effects=True, vmem_limit_bytes=67043328
        ),
    )(ids, gates, klat, krope, tok, qn, qr, ku, vu, gw, uw, dw)
    return att, rout


def solution(mesh):
    body = functools.partial(local, mesh.shape["ctx"], mesh.shape["sec"])
    both = ("ctx", "sec")
    return jax.shard_map(
        body,
        mesh=mesh,
        in_specs=(
            P("ctx", "sec"),
            P("ctx", "sec"),
            P("ctx", None),
            P("ctx", None),
            P("sec", None, None),
            P("sec", None, None),
            P(both, None),
            P(both, None),
            P(both, None),
            P(None, both),
            P(None, both),
            P(both, None),
        ),
        out_specs=(P("ctx", "sec"), P(both, None)),
        check_vma=False,
    )
```

```python
import functools

import jax
import jax.numpy as jnp
from jax import lax
from jax.experimental import pallas as pl
from jax.experimental.pallas import tpu as pltpu
from jax.sharding import PartitionSpec as P

CAP = 4
SPLIT = 8
CHUNKS = 4
LOG2E = 1.4426950408889634
MESH_ID = pl.DeviceIdType.MESH
F32 = jnp.float32
BF16 = jnp.bfloat16
NT = (((1,), (1,)), ((), ()))


def kernel(
    dims,
    ids_ref,
    gates_ref,
    klat_ref,
    krope_ref,
    tok_hbm,
    qn_hbm,
    qr_hbm,
    ku_hbm,
    vu_hbm,
    gw_hbm,
    uw_hbm,
    dw_hbm,
    att_ref,
    resb,
    wmix,
    tok,
    qn,
    qr,
    ku,
    vu,
    gw,
    uw,
    dw,
    qcat,
    keys,
    outg,
    zbuf,
    arr,
    acc,
    part,
    r1,
    s1,
    r2,
    s2,
    r3,
    rbuf,
    load_sem,
    kz_send,
    kx_send,
    ky_send,
    kc_send,
    krecv,
    zsend,
    zrecv,
    asend,
    arecv,
    rsend,
    rrecv,
    bsend,
    brecv,
):
    groups, n_sec, rows, heads, lat, ropew, nope, hb = dims
    slots = groups * CAP
    width = tok.shape[1]
    cw = width // CHUNKS
    tokens = tok.shape[0]
    sent = lat + 2 * ropew
    ctx = lax.axis_index("ctx")
    sec = lax.axis_index("sec")
    me = ctx * n_sec + sec
    g = me // SPLIT
    m = lax.rem(me, SPLIT)
    bx = lax.rem(m, 2)
    bc = lax.rem(m // 2, 2)
    by = m // 4
    mx = m + 1 - 2 * bx
    mc = m + 2 - 4 * bc
    my = m + 4 - 8 * by
    mxy = mx + my - m

    def dev(group, member):
        index = group * SPLIT + member
        return (index // n_sec, lax.rem(index, n_sec))

    pending = []

    def rcopy(src, dst, ss, rs, target):
        return pltpu.make_async_remote_copy(
            src_ref=src, dst_ref=dst, send_sem=ss, recv_sem=rs,
            device_id=target, device_id_type=MESH_ID,
        )

    def send(src, dst, ss, rs, target):
        cp = rcopy(src, dst, ss, rs, target)
        cp.start()
        pending.append(cp)
        return cp

    nx, nc, ny = dev(g, mx), dev(g, mc), dev(g, my)
    others = [lax.rem(g + step, groups) for step in range(1, groups)]
    every = [g] + others

    barrier = pltpu.get_barrier_semaphore()
    for target in [nx, nc, ny] + [dev(o, m) for o in others]:
        pl.semaphore_signal(barrier, inc=1, device_id=target, device_id_type=MESH_ID)

    pairs = [
        (tok_hbm, tok), (qn_hbm, qn), (qr_hbm, qr), (ku_hbm, ku),
        (gw_hbm, gw), (uw_hbm, uw), (dw_hbm, dw), (vu_hbm, vu),
    ]
    loads = [pltpu.make_async_copy(a, b, load_sem.at[i]) for i, (a, b) in enumerate(pairs)]
    for load in loads:
        load.start()

    lanes = wmix.shape[1]
    row = lax.broadcasted_iota(jnp.int32, (lanes, tokens), 0)
    slot = row & (slots - 1)
    expert = slot // CAP
    matches = jnp.zeros((lanes, tokens), F32)
    gate = jnp.zeros((lanes, tokens), F32)
    for k in range(ids_ref.shape[0]):
        hit = ids_ref[k : k + 1, :] == expert
        matches = jnp.where(hit, 1.0, matches)
        gate = gate + jnp.where(hit, gates_ref[k : k + 1, :], 0.0)
    earlier = (
        lax.broadcasted_iota(jnp.int32, (tokens, tokens), 0)
        < lax.broadcasted_iota(jnp.int32, (tokens, tokens), 1)
    )
    rank = jnp.dot(
        matches.astype(BF16), jnp.where(earlier, 1.0, 0.0).astype(BF16), preferred_element_type=F32
    )
    chosen = jnp.where(rank == (slot & (CAP - 1)).astype(F32), matches, 0.0)
    picker = chosen[:slots].astype(BF16)

    own_keys = keys.at[ctx]
    own_keys[:, :lat] = klat_ref[...]
    own_keys[:, lat:sent] = jnp.concatenate([krope_ref[...], krope_ref[...]], axis=1)

    loads[0].wait()
    for c in range(CHUNKS):
        picked = jnp.dot(picker, tok[:, c * cw : (c + 1) * cw], preferred_element_type=F32)
        for e in range(groups):
            outg[c, e] = picked[e * CAP : (e + 1) * CAP].astype(BF16)
        if c == 0:
            pl.semaphore_wait(barrier, 3 + len(others))
        for i, o in enumerate(others):
            send(outg.at[c, o], zbuf.at[c, g], zsend.at[c, i], zrecv.at[c, g], dev(o, m))

    part_rows = rows // 2

    def kpiece(shard, which):
        return keys.at[shard, pl.ds(pl.multiple_of(which * part_rows, part_rows), part_rows), pl.ds(0, sent)]

    def kwhole(shard):
        return keys.at[shard, :, pl.ds(0, sent)]

    def kshard(group, member):
        return (group * SPLIT + member) // n_sec

    def ksend(group, member, sem, target):
        shard = kshard(group, member)
        piece = kpiece(shard, bx)
        send(piece, piece, sem, krecv.at[shard, bx], target)

    def karrive(group, member, which):
        shard = kshard(group, member)
        piece = kpiece(shard, which)
        rcopy(piece, piece, kz_send.at[0], krecv.at[shard, which], nx).wait_recv()

    for i, o in enumerate(others):
        ksend(g, m, kz_send.at[i], dev(o, m))

    weight = chosen * gate
    w1 = weight.astype(BF16).astype(F32)
    w2 = (weight - w1).astype(BF16).astype(F32)
    w3 = weight - w1 - w2
    wmix[...] = jnp.where(
        row < slots, w1, jnp.where(row < 2 * slots, w2, jnp.where(row < 3 * slots, w3, 0.0))
    ).T.astype(BF16)

    maskw = keys.shape[2] - sent

    @pl.loop(0, keys.shape[0])
    def _(shard):
        key_place = shard * rows + lax.broadcasted_iota(jnp.int32, (rows, maskw), 0)
        query = lax.broadcasted_iota(jnp.int32, (rows, maskw), 1)
        hidden_key = (key_place > ctx * rows + query) & (query < rows)
        keys[shard, :, sent:] = jnp.where(hidden_key, -1e30, 0.0).astype(BF16)

    loads[1].wait()
    loads[2].wait()
    loads[3].wait()
    unit = jnp.where(
        lax.broadcasted_iota(jnp.int32, (rows, maskw), 0)
        == lax.broadcasted_iota(jnp.int32, (rows, maskw), 1),
        1.0,
        0.0,
    ).astype(BF16)

    def query_latents(first, last):
        @pl.loop(first, last)
        def _(p):
            rope = qr[:, pl.ds(pl.multiple_of(p * 2 * ropew, 2 * ropew), 2 * ropew)]
            low = lax.broadcasted_iota(jnp.int32, rope.shape, 1) < ropew
            for k in range(2):
                h = p * 2 + k
                q = qn[:, pl.ds(pl.multiple_of(h * nope, nope), nope)]
                latent = lax.dot_general(q, ku[h], NT, preferred_element_type=F32)
                place = pl.ds(pl.multiple_of(h * rows, rows), rows)
                qcat[place, :lat] = latent.astype(BF16)
                keep = low if k == 0 else jnp.logical_not(low)
                qcat[place, lat:sent] = jnp.where(keep, rope.astype(F32), 0.0).astype(BF16)
                qcat[place, sent:] = unit

    half_pairs = heads // 4
    query_latents(0, half_pairs)

    def spread(kind, member, c, target):
        piece = arr.at[c, member]
        send(piece, piece, asend.at[kind, c], arecv.at[c, member], target)

    def arrive(member, c):
        piece = arr.at[c, member]
        rcopy(piece, piece, asend.at[0, c], arecv.at[c, member], nx).wait_recv()

    def start_chunk(c):
        for i, o in enumerate(others):
            rcopy(outg.at[c, o], zbuf.at[c, o], zsend.at[c, i], zrecv.at[c, o], dev(o, m)).wait_recv()
        zbuf[c, g] = outg[c, g]
        blocks = [zbuf[c, e].astype(F32) for e in range(groups)]
        arr[c, m] = jnp.concatenate(blocks, axis=0).astype(BF16)
        spread(0, m, c, nx)
        spread(1, m, c, ny)
        spread(2, m, c, nc)

    def forward_chunk(c):
        arrive(mx, c)
        if c % 2 == 0:
            spread(3, mx, c, ny)
        spread(4, mx, c, nc)
        arrive(my, c)
        if c % 2 == 1:
            spread(3, my, c, nx)
        spread(5, my, c, nc)

    count = SPLIT * slots

    def finish_chunk(c):
        arrive(mxy, c)
        spread(6, mxy, c, nc)

    def gate_up(c):
        for member in (mc, mx + mc - m, my + mc - m, mxy + mc - m):
            arrive(member, c)
        x = arr[c].reshape(count, cw)
        g_part = jnp.dot(x, gw[c * cw : (c + 1) * cw], preferred_element_type=F32)
        u_part = jnp.dot(x, uw[c * cw : (c + 1) * cw], preferred_element_type=F32)
        if c == 0:
            acc[0] = g_part
            acc[1] = u_part
        else:
            acc[0] += g_part
            acc[1] += u_part

    start_chunk(0)
    start_chunk(1)
    forward_chunk(0)
    start_chunk(2)
    forward_chunk(1)
    start_chunk(3)
    finish_chunk(0)
    forward_chunk(2)
    finish_chunk(1)
    forward_chunk(3)

    ksend(g, m, ky_send.at[0], ny)
    for i, o in enumerate(others):
        karrive(o, m, bx)
        ksend(o, m, kx_send.at[i, 0], nx)
        ksend(o, m, ky_send.at[i + 1], ny)

    loads[4].wait()
    loads[5].wait()
    gate_up(0)
    finish_chunk(2)
    gate_up(1)
    finish_chunk(3)
    query_latents(half_pairs, heads // 2)
    gate_up(2)
    gate_up(3)
    gate_act = acc[0]
    hidden = (gate_act / (1.0 + jnp.exp(-gate_act)) * acc[1]).astype(BF16)

    c1, c2, c3 = [], [], []
    loads[6].wait()

    def down(c):
        value = jnp.dot(hidden, dw[:, c * cw : (c + 1) * cw], preferred_element_type=F32)
        part[c] = value.astype(BF16).reshape(2, 2, 2, slots, cw)
        c1.append(send(part.at[c, :, 1 - bc], r1.at[c], rsend.at[0, c], rrecv.at[0, c], nc))

    def sum_cores(c):
        c1[c].wait_recv()
        for a in range(2):
            for b in range(2):
                s1[c, a, b] = (part[c, a, bc, b].astype(F32) + r1[c, a, b].astype(F32)).astype(BF16)
        src = s1.at[c, :, 1 - bx] if c % 2 == 0 else s1.at[c, 1 - by]
        c2.append(send(src, r2.at[c], rsend.at[1, c], rrecv.at[1, c], nx if c % 2 == 0 else ny))

    def sum_first(c):
        c2[c].wait_recv()
        for a in range(2):
            mine = s1[c, a, bx] if c % 2 == 0 else s1[c, by, a]
            s2[c, a] = (mine.astype(F32) + r2[c, a].astype(F32)).astype(BF16)
        keep = by if c % 2 == 0 else bx
        c3.append(send(s2.at[c, 1 - keep], r3.at[c], rsend.at[2, c], rrecv.at[2, c],
                       ny if c % 2 == 0 else nx))

    def sum_second(c):
        c3[c].wait_recv()
        keep = by if c % 2 == 0 else bx
        total = s2[c, keep].astype(F32) + r3[c].astype(F32)
        for e in range(groups):
            rbuf[c, e] = total[e * CAP : (e + 1) * CAP].astype(BF16)
        for i, o in enumerate(others):
            send(rbuf.at[c, o], resb.at[c, g], bsend.at[c, i], brecv.at[c, g], dev(o, m))
        resb[c, g] = rbuf[c, g]

    down(0)
    down(1)
    down(2)
    sum_cores(0)
    down(3)
    sum_cores(1)
    sum_cores(2)
    sum_cores(3)

    for i, o in enumerate(every):
        karrive(o, my, bx)
        ksend(o, my, kx_send.at[i, 1], nx)
    shard = kshard(g, m)
    send(kwhole(shard), kwhole(shard), kc_send.at[0, 0], krecv.at[kshard(g, m), 0], nc)
    for i, o in enumerate(others):
        karrive(o, m, 1 - bx)
        shard = kshard(o, m)
        send(kwhole(shard), kwhole(shard), kc_send.at[i + 1, 0], krecv.at[shard, 0], nc)
    sum_first(0)
    sum_first(1)
    for i, o in enumerate(every):
        karrive(o, my, 1 - bx)
        shard = kshard(o, my)
        send(kwhole(shard), kwhole(shard), kc_send.at[i, 1], krecv.at[shard, 0], nc)
    loads[7].wait()
    for o in every:
        for member in (mc, my + mc - m):
            shard = kshard(o, member)
            rcopy(kwhole(shard), kwhole(shard), kc_send.at[0, 0], krecv.at[shard, 0], nc).wait_recv()

    seq = keys.shape[0] * keys.shape[1]
    block = hb * rows
    scale = (nope + ropew) ** -0.5 * LOG2E

    def attend(first, last):
        @pl.loop(first, last)
        def _(b):
            q = qcat[pl.ds(pl.multiple_of(b * block, block), block)]
            kk = keys[...].reshape(seq, keys.shape[2])
            score = lax.dot_general(q, kk, NT, preferred_element_type=F32)
            top = jnp.max(score, axis=1, keepdims=True)
            expo = jnp.exp2((score - top) * scale)
            total = jnp.sum(expo, axis=1, keepdims=True)
            mixed = jnp.dot(expo.astype(BF16), kk[:, :lat], preferred_element_type=F32)
            mixed = (mixed / total).astype(BF16)
            for k in range(hb):
                h = b * hb + k
                value = jnp.dot(
                    mixed[k * rows : (k + 1) * rows], vu[h], preferred_element_type=F32
                )
                vdim = value.shape[1]
                att_ref[:, pl.ds(pl.multiple_of(h * vdim, vdim), vdim)] = value.astype(BF16)

    nb = heads // hb
    eighth = nb // 8
    sum_first(2)
    sum_first(3)
    attend(0, eighth)
    sum_second(0)
    sum_second(1)
    attend(eighth, 2 * eighth)
    sum_second(2)
    sum_second(3)
    attend(2 * eighth, nb)

    for c in range(CHUNKS):
        for i, o in enumerate(others):
            rcopy(rbuf.at[c, o], resb.at[c, o], bsend.at[c, i], brecv.at[c, o], dev(o, m)).wait_recv()
    for cp in pending:
        cp.wait_send()


def finish(res_ref, wmix_ref, att_in, rout_ref, att_out):
    groups = res_ref.shape[1]
    block_rows = jnp.concatenate([res_ref[0, e].astype(F32) for e in range(groups)], axis=0)
    times = wmix_ref.shape[1] // block_rows.shape[0]
    tall = jnp.concatenate([block_rows] * times, axis=0).astype(BF16)
    rout_ref[...] = jnp.dot(wmix_ref[...], tall, preferred_element_type=F32).astype(BF16)
    att_out[...] = att_in[...]


def local(n_ctx, n_sec, qn, qr, klat, krope, ku, vu, tok, ids, gates, gw, uw, dw):
    devices = n_ctx * n_sec
    groups = devices // SPLIT
    slots = groups * CAP
    rows = qn.shape[0]
    heads, lat, nope = ku.shape
    ropew = krope.shape[1]
    tokens, width = tok.shape
    cw = width // CHUNKS
    kw = lat + 2 * ropew + 128
    hb = 4 if n_ctx * rows <= 2048 else 1
    lanes = -(-3 * slots // 128) * 128
    dims = (groups, n_sec, rows, heads, lat, ropew, nope, hb)
    v = pl.BlockSpec(memory_space=pltpu.VMEM)
    a = pl.BlockSpec(memory_space=pl.ANY)
    dma = pltpu.SemaphoreType.DMA
    out_width = heads * vu.shape[2]
    att, res, wmix = pl.pallas_call(
        functools.partial(kernel, dims),
        out_shape=(
            jax.ShapeDtypeStruct((rows, out_width), BF16),
            jax.ShapeDtypeStruct((CHUNKS, groups, CAP, cw), BF16),
            jax.ShapeDtypeStruct((tokens, lanes), BF16),
        ),
        in_specs=[v, v, v, v] + [a] * 8,
        out_specs=(v, v, v),
        scratch_shapes=[
            pltpu.VMEM(tok.shape, BF16),
            pltpu.VMEM(qn.shape, BF16),
            pltpu.VMEM(qr.shape, BF16),
            pltpu.VMEM(ku.shape, BF16),
            pltpu.VMEM(vu.shape, BF16),
            pltpu.VMEM(gw.shape, BF16),
            pltpu.VMEM(uw.shape, BF16),
            pltpu.VMEM(dw.shape, BF16),
            pltpu.VMEM((heads * rows, kw), BF16),
            pltpu.VMEM((n_ctx, rows, kw), BF16),
            pltpu.VMEM((CHUNKS, groups, CAP, cw), BF16),
            pltpu.VMEM((CHUNKS, groups, CAP, cw), BF16),
            pltpu.VMEM((CHUNKS, SPLIT, slots, cw), BF16),
            pltpu.VMEM((2, SPLIT * slots, gw.shape[1]), F32),
            pltpu.VMEM((CHUNKS, 2, 2, 2, slots, cw), BF16),
            pltpu.VMEM((CHUNKS, 2, 2, slots, cw), BF16),
            pltpu.VMEM((CHUNKS, 2, 2, slots, cw), BF16),
            pltpu.VMEM((CHUNKS, 2, slots, cw), BF16),
            pltpu.VMEM((CHUNKS, 2, slots, cw), BF16),
            pltpu.VMEM((CHUNKS, slots, cw), BF16),
            pltpu.VMEM((CHUNKS, groups, CAP, cw), BF16),
            dma((8,)),
            dma((groups,)),
            dma((groups, 2)),
            dma((groups,)),
            dma((groups, 2)),
            dma((n_ctx, 2)),
            dma((CHUNKS, groups)),
            dma((CHUNKS, groups)),
            dma((7, CHUNKS)),
            dma((CHUNKS, SPLIT)),
            dma((3, CHUNKS)),
            dma((3, CHUNKS)),
            dma((CHUNKS, groups)),
            dma((CHUNKS, groups)),
        ],
        compiler_params=pltpu.CompilerParams(
            collective_id=0, has_side_effects=True, vmem_limit_bytes=67043328
        ),
    )(ids.T, gates.T, klat, krope, tok, qn, qr, ku, vu, gw, uw, dw)
    rout, att = pl.pallas_call(
        finish,
        grid=(CHUNKS,),
        out_shape=(jax.ShapeDtypeStruct(tok.shape, BF16), jax.ShapeDtypeStruct(att.shape, BF16)),
        in_specs=[
            pl.BlockSpec((1, groups, CAP, cw), lambda i: (i, 0, 0, 0)),
            pl.BlockSpec((tokens, lanes), lambda i: (0, 0)),
            pl.BlockSpec((rows, out_width // CHUNKS), lambda i: (0, i)),
        ],
        out_specs=(
            pl.BlockSpec((tokens, cw), lambda i: (0, i)),
            pl.BlockSpec((rows, out_width // CHUNKS), lambda i: (0, i)),
        ),
    )(res, wmix, att)
    return att, rout


def solution(mesh):
    body = functools.partial(local, mesh.shape["ctx"], mesh.shape["sec"])
    both = ("ctx", "sec")
    return jax.shard_map(
        body,
        mesh=mesh,
        in_specs=(
            P("ctx", "sec"),
            P("ctx", "sec"),
            P("ctx", None),
            P("ctx", None),
            P("sec", None, None),
            P("sec", None, None),
            P(both, None),
            P(both, None),
            P(both, None),
            P(None, both),
            P(None, both),
            P(both, None),
        ),
        out_specs=(P("ctx", "sec"), P(both, None)),
        check_vma=False,
    )
```

```python
import functools

import jax
import jax.numpy as jnp
from jax import lax
from jax.experimental import pallas as pl
from jax.experimental.pallas import tpu as pltpu
from jax.sharding import PartitionSpec as P

CAP = 4
SPLIT = 8
CHUNKS = 4
LOG2E = 1.4426950408889634
MESH_ID = pl.DeviceIdType.MESH
F32 = jnp.float32
BF16 = jnp.bfloat16
NT = (((1,), (1,)), ((), ()))


def kernel(
    dims,
    ids_ref,
    gates_ref,
    klat_ref,
    krope_ref,
    tok_hbm,
    qn_hbm,
    qr_hbm,
    ku_hbm,
    vu_hbm,
    gw_hbm,
    uw_hbm,
    dw_hbm,
    att_ref,
    resb,
    wmix,
    tok,
    qn,
    qr,
    ku,
    vu,
    gw,
    uw,
    dw,
    qcat,
    keys,
    outg,
    zbuf,
    arr,
    acc,
    part,
    r1,
    s1,
    r2,
    s2,
    r3,
    rbuf,
    load_sem,
    kz_send,
    kx_send,
    ky_send,
    kc_send,
    krecv,
    zsend,
    zrecv,
    asend,
    arecv,
    rsend,
    rrecv,
    bsend,
    brecv,
):
    groups, n_sec, rows, heads, lat, ropew, nope, hb = dims
    slots = groups * CAP
    width = tok.shape[1]
    cw = width // CHUNKS
    tokens = tok.shape[0]
    sent = lat + 2 * ropew
    ctx = lax.axis_index("ctx")
    sec = lax.axis_index("sec")
    me = ctx * n_sec + sec
    g = me // SPLIT
    m = lax.rem(me, SPLIT)
    bx = lax.rem(m, 2)
    bc = lax.rem(m // 2, 2)
    by = m // 4
    mx = m + 1 - 2 * bx
    mc = m + 2 - 4 * bc
    my = m + 4 - 8 * by
    mxy = mx + my - m

    def dev(group, member):
        index = group * SPLIT + member
        return (index // n_sec, lax.rem(index, n_sec))

    pending = []

    def rcopy(src, dst, ss, rs, target):
        return pltpu.make_async_remote_copy(
            src_ref=src, dst_ref=dst, send_sem=ss, recv_sem=rs,
            device_id=target, device_id_type=MESH_ID,
        )

    def send(src, dst, ss, rs, target):
        cp = rcopy(src, dst, ss, rs, target)
        cp.start()
        pending.append(cp)
        return cp

    nx, nc, ny = dev(g, mx), dev(g, mc), dev(g, my)
    others = [lax.rem(g + step, groups) for step in range(1, groups)]
    every = [g] + others

    tok_loads = []
    for c in range(CHUNKS):
        cols = pl.ds(c * cw, cw)
        tok_loads.append(
            pltpu.make_async_copy(tok_hbm.at[:, cols], tok.at[:, cols], load_sem.at[8 + c])
        )
        tok_loads[c].start()

    barrier = pltpu.get_barrier_semaphore()
    for target in [nx, nc, ny] + [dev(o, m) for o in others]:
        pl.semaphore_signal(barrier, inc=1, device_id=target, device_id_type=MESH_ID)

    pairs = [
        (qn_hbm, qn), (qr_hbm, qr), (ku_hbm, ku),
        (gw_hbm, gw), (uw_hbm, uw), (dw_hbm, dw), (vu_hbm, vu),
    ]
    loads = [None]
    for i, (a, b) in enumerate(pairs):
        loads.append(pltpu.make_async_copy(a, b, load_sem.at[i]))

    own_keys = keys.at[ctx]
    own_keys[:, :lat] = klat_ref[...]
    own_keys[:, lat:sent] = jnp.concatenate([krope_ref[...], krope_ref[...]], axis=1)

    pl.semaphore_wait(barrier, 3 + len(others))
    part_rows = rows // 2

    def kpiece(shard, which):
        return keys.at[shard, pl.ds(pl.multiple_of(which * part_rows, part_rows), part_rows), pl.ds(0, sent)]

    def kwhole(shard):
        return keys.at[shard, :, pl.ds(0, sent)]

    def kshard(group, member):
        return (group * SPLIT + member) // n_sec

    def ksend(group, member, which, sem, target):
        shard = kshard(group, member)
        piece = kpiece(shard, which)
        send(piece, piece, sem, krecv.at[shard, which], target)

    def karrive(group, member, which):
        shard = kshard(group, member)
        piece = kpiece(shard, which)
        rcopy(piece, piece, kz_send.at[0], krecv.at[shard, which], nx).wait_recv()

    for i, o in enumerate(others):
        ksend(g, m, bx, kz_send.at[i], dev(o, m))
    for which in range(2):
        ksend(g, m, which, kz_send.at[groups - 1 + which], ny)

    lanes = wmix.shape[1]
    row = lax.broadcasted_iota(jnp.int32, (lanes, tokens), 0)
    slot = row & (slots - 1)
    expert = slot // CAP
    matches = jnp.zeros((lanes, tokens), F32)
    gate = jnp.zeros((lanes, tokens), F32)
    for k in range(ids_ref.shape[0]):
        hit = ids_ref[k : k + 1, :] == expert
        matches = jnp.where(hit, 1.0, matches)
        gate = gate + jnp.where(hit, gates_ref[k : k + 1, :], 0.0)
    earlier = (
        lax.broadcasted_iota(jnp.int32, (tokens, tokens), 0)
        < lax.broadcasted_iota(jnp.int32, (tokens, tokens), 1)
    )
    rank = jnp.dot(
        matches.astype(BF16), jnp.where(earlier, 1.0, 0.0).astype(BF16), preferred_element_type=F32
    )
    chosen = jnp.where(rank == (slot & (CAP - 1)).astype(F32), matches, 0.0)
    picker = chosen[:slots].astype(BF16)

    for c in range(CHUNKS):
        tok_loads[c].wait()
        picked = jnp.dot(picker, tok[:, c * cw : (c + 1) * cw], preferred_element_type=F32)
        for e in range(groups):
            outg[c, e] = picked[e * CAP : (e + 1) * CAP].astype(BF16)
        for i, o in enumerate(others):
            send(outg.at[c, o], zbuf.at[c, g], zsend.at[c, i], zrecv.at[c, g], dev(o, m))

    for load in loads[1:4]:
        load.start()
    weight = chosen * gate
    w1 = weight.astype(BF16).astype(F32)
    w2 = (weight - w1).astype(BF16).astype(F32)
    w3 = weight - w1 - w2
    wmix[...] = jnp.where(
        row < slots, w1, jnp.where(row < 2 * slots, w2, jnp.where(row < 3 * slots, w3, 0.0))
    ).T.astype(BF16)

    maskw = keys.shape[2] - sent

    @pl.loop(0, keys.shape[0])
    def _(shard):
        key_place = shard * rows + lax.broadcasted_iota(jnp.int32, (rows, maskw), 0)
        query = lax.broadcasted_iota(jnp.int32, (rows, maskw), 1)
        hidden_key = (key_place > ctx * rows + query) & (query < rows)
        keys[shard, :, sent:] = jnp.where(hidden_key, -1e30, 0.0).astype(BF16)

    loads[1].wait()
    loads[2].wait()
    loads[3].wait()
    for load in loads[4:]:
        load.start()
    unit = jnp.where(
        lax.broadcasted_iota(jnp.int32, (rows, maskw), 0)
        == lax.broadcasted_iota(jnp.int32, (rows, maskw), 1),
        1.0,
        0.0,
    ).astype(BF16)

    def query_latents(first, last):
        @pl.loop(first, last)
        def _(p):
            rope = qr[:, pl.ds(pl.multiple_of(p * 2 * ropew, 2 * ropew), 2 * ropew)]
            low = lax.broadcasted_iota(jnp.int32, rope.shape, 1) < ropew
            for k in range(2):
                h = p * 2 + k
                q = qn[:, pl.ds(pl.multiple_of(h * nope, nope), nope)]
                latent = lax.dot_general(q, ku[h], NT, preferred_element_type=F32)
                place = pl.ds(pl.multiple_of(h * rows, rows), rows)
                qcat[place, :lat] = latent.astype(BF16)
                keep = low if k == 0 else jnp.logical_not(low)
                qcat[place, lat:sent] = jnp.where(keep, rope.astype(F32), 0.0).astype(BF16)
                qcat[place, sent:] = unit

    half_pairs = heads // 4
    query_latents(0, half_pairs)

    for i, o in enumerate(others):
        karrive(o, m, bx)
        ksend(o, m, bx, kx_send.at[i, 0], nx)
        ksend(o, m, bx, ky_send.at[i], ny)

    def spread(kind, member, c, target):
        piece = arr.at[c, member]
        send(piece, piece, asend.at[kind, c], arecv.at[c, member], target)

    def arrive(member, c):
        piece = arr.at[c, member]
        rcopy(piece, piece, asend.at[0, c], arecv.at[c, member], nx).wait_recv()

    def start_chunk(c):
        for i, o in enumerate(others):
            rcopy(outg.at[c, o], zbuf.at[c, o], zsend.at[c, i], zrecv.at[c, o], dev(o, m)).wait_recv()
        zbuf[c, g] = outg[c, g]
        blocks = [zbuf[c, e].astype(F32) for e in range(groups)]
        arr[c, m] = jnp.concatenate(blocks, axis=0).astype(BF16)
        spread(0, m, c, nx)
        spread(1, m, c, ny)
        spread(2, m, c, nc)

    def forward_chunk(c):
        arrive(mx, c)
        if c % 2 == 0:
            spread(3, mx, c, ny)
        spread(4, mx, c, nc)
        arrive(my, c)
        if c % 2 == 1:
            spread(3, my, c, nx)
        spread(5, my, c, nc)

    count = SPLIT * slots

    def finish_chunk(c):
        arrive(mxy, c)
        spread(6, mxy, c, nc)

    def gate_up(c):
        for member in (mc, mx + mc - m, my + mc - m, mxy + mc - m):
            arrive(member, c)
        x = arr[c].reshape(count, cw)
        g_part = jnp.dot(x, gw[c * cw : (c + 1) * cw], preferred_element_type=F32)
        u_part = jnp.dot(x, uw[c * cw : (c + 1) * cw], preferred_element_type=F32)
        if c == 0:
            acc[0] = g_part
            acc[1] = u_part
        else:
            acc[0] += g_part
            acc[1] += u_part

    start_chunk(0)
    start_chunk(1)
    for i, o in enumerate(others):
        karrive(o, my, bx)
        ksend(o, my, bx, kx_send.at[i, 1], nx)
    forward_chunk(0)
    start_chunk(2)
    forward_chunk(1)
    start_chunk(3)
    finish_chunk(0)
    forward_chunk(2)
    finish_chunk(1)
    forward_chunk(3)

    shard = kshard(g, m)
    send(kwhole(shard), kwhole(shard), kc_send.at[0, 0], krecv.at[shard, 0], nc)
    for i, o in enumerate(others):
        karrive(o, m, 1 - bx)
        shard = kshard(o, m)
        send(kwhole(shard), kwhole(shard), kc_send.at[i + 1, 0], krecv.at[shard, 0], nc)
    for i, o in enumerate(every):
        karrive(o, my, 1 - bx)
        if i == 0:
            karrive(o, my, bx)
        shard = kshard(o, my)
        send(kwhole(shard), kwhole(shard), kc_send.at[i, 1], krecv.at[shard, 0], nc)

    loads[4].wait()
    loads[5].wait()
    gate_up(0)
    finish_chunk(2)
    gate_up(1)
    finish_chunk(3)
    query_latents(half_pairs, heads // 2)
    gate_up(2)
    gate_up(3)
    gate_act = acc[0]
    hidden = (gate_act / (1.0 + jnp.exp(-gate_act)) * acc[1]).astype(BF16)

    c1, c2, c3 = [], [], []
    loads[6].wait()

    def down(c):
        value = jnp.dot(hidden, dw[:, c * cw : (c + 1) * cw], preferred_element_type=F32)
        part[c] = value.astype(BF16).reshape(2, 2, 2, slots, cw)
        c1.append(send(part.at[c, :, 1 - bc], r1.at[c], rsend.at[0, c], rrecv.at[0, c], nc))

    def sum_cores(c):
        c1[c].wait_recv()
        for a in range(2):
            for b in range(2):
                s1[c, a, b] = (part[c, a, bc, b].astype(F32) + r1[c, a, b].astype(F32)).astype(BF16)
        src = s1.at[c, :, 1 - bx] if c % 2 == 0 else s1.at[c, 1 - by]
        c2.append(send(src, r2.at[c], rsend.at[1, c], rrecv.at[1, c], nx if c % 2 == 0 else ny))

    def sum_first(c):
        c2[c].wait_recv()
        for a in range(2):
            mine = s1[c, a, bx] if c % 2 == 0 else s1[c, by, a]
            s2[c, a] = (mine.astype(F32) + r2[c, a].astype(F32)).astype(BF16)
        keep = by if c % 2 == 0 else bx
        c3.append(send(s2.at[c, 1 - keep], r3.at[c], rsend.at[2, c], rrecv.at[2, c],
                       ny if c % 2 == 0 else nx))

    def sum_second(c):
        c3[c].wait_recv()
        keep = by if c % 2 == 0 else bx
        total = s2[c, keep].astype(F32) + r3[c].astype(F32)
        for e in range(groups):
            rbuf[c, e] = total[e * CAP : (e + 1) * CAP].astype(BF16)
        for i, o in enumerate(others):
            send(rbuf.at[c, o], resb.at[c, g], bsend.at[c, i], brecv.at[c, g], dev(o, m))
        resb[c, g] = rbuf[c, g]

    for c in range(CHUNKS):
        down(c)

    loads[7].wait()
    for o in every:
        for member in (mc, my + mc - m):
            shard = kshard(o, member)
            rcopy(kwhole(shard), kwhole(shard), kc_send.at[0, 0], krecv.at[shard, 0], nc).wait_recv()

    seq = keys.shape[0] * keys.shape[1]
    block = hb * rows
    scale = (nope + ropew) ** -0.5 * LOG2E

    def attend(first, last):
        @pl.loop(first, last)
        def _(b):
            q = qcat[pl.ds(pl.multiple_of(b * block, block), block)]
            kk = keys[...].reshape(seq, keys.shape[2])
            score = lax.dot_general(q, kk, NT, preferred_element_type=F32)
            top = jnp.max(score, axis=1, keepdims=True)
            expo = jnp.exp2((score - top) * scale)
            total = jnp.sum(expo, axis=1, keepdims=True)
            mixed = jnp.dot(expo.astype(BF16), kk[:, :lat], preferred_element_type=F32)
            mixed = (mixed / total).astype(BF16)
            for k in range(hb):
                h = b * hb + k
                value = jnp.dot(
                    mixed[k * rows : (k + 1) * rows], vu[h], preferred_element_type=F32
                )
                vdim = value.shape[1]
                att_ref[:, pl.ds(pl.multiple_of(h * vdim, vdim), vdim)] = value.astype(BF16)

    nb = heads // hb
    eighth = nb // 8
    attend(0, eighth)
    for c in range(CHUNKS):
        sum_cores(c)
    attend(eighth, 3 * eighth)
    for c in range(CHUNKS):
        sum_first(c)
    attend(3 * eighth, 5 * eighth)
    for c in range(CHUNKS):
        sum_second(c)
    attend(5 * eighth, nb)

    for c in range(CHUNKS):
        for i, o in enumerate(others):
            rcopy(rbuf.at[c, o], resb.at[c, o], bsend.at[c, i], brecv.at[c, o], dev(o, m)).wait_recv()
    for cp in pending:
        cp.wait_send()


def finish(res_ref, wmix_ref, att_in, rout_ref, att_out):
    groups = res_ref.shape[1]
    block_rows = jnp.concatenate([res_ref[0, e].astype(F32) for e in range(groups)], axis=0)
    block_rows = block_rows.astype(BF16)
    tall = jnp.concatenate([block_rows] * 3, axis=0)
    rout_ref[...] = jnp.dot(
        wmix_ref[:, : tall.shape[0]], tall, preferred_element_type=F32
    ).astype(BF16)
    att_out[...] = att_in[...]


def local(n_ctx, n_sec, qn, qr, klat, krope, ku, vu, tok, ids, gates, gw, uw, dw):
    devices = n_ctx * n_sec
    groups = devices // SPLIT
    slots = groups * CAP
    rows = qn.shape[0]
    heads, lat, nope = ku.shape
    ropew = krope.shape[1]
    tokens, width = tok.shape
    cw = width // CHUNKS
    kw = lat + 2 * ropew + 128
    hb = 4 if n_ctx * rows <= 2048 else 1
    lanes = -(-3 * slots // 128) * 128
    dims = (groups, n_sec, rows, heads, lat, ropew, nope, hb)
    v = pl.BlockSpec(memory_space=pltpu.VMEM)
    a = pl.BlockSpec(memory_space=pl.ANY)
    dma = pltpu.SemaphoreType.DMA
    out_width = heads * vu.shape[2]
    att, res, wmix = pl.pallas_call(
        functools.partial(kernel, dims),
        out_shape=(
            jax.ShapeDtypeStruct((rows, out_width), BF16),
            jax.ShapeDtypeStruct((CHUNKS, groups, CAP, cw), BF16),
            jax.ShapeDtypeStruct((tokens, lanes), BF16),
        ),
        in_specs=[v, v, v, v] + [a] * 8,
        out_specs=(v, v, v),
        scratch_shapes=[
            pltpu.VMEM(tok.shape, BF16),
            pltpu.VMEM(qn.shape, BF16),
            pltpu.VMEM(qr.shape, BF16),
            pltpu.VMEM(ku.shape, BF16),
            pltpu.VMEM(vu.shape, BF16),
            pltpu.VMEM(gw.shape, BF16),
            pltpu.VMEM(uw.shape, BF16),
            pltpu.VMEM(dw.shape, BF16),
            pltpu.VMEM((heads * rows, kw), BF16),
            pltpu.VMEM((n_ctx, rows, kw), BF16),
            pltpu.VMEM((CHUNKS, groups, CAP, cw), BF16),
            pltpu.VMEM((CHUNKS, groups, CAP, cw), BF16),
            pltpu.VMEM((CHUNKS, SPLIT, slots, cw), BF16),
            pltpu.VMEM((2, SPLIT * slots, gw.shape[1]), F32),
            pltpu.VMEM((CHUNKS, 2, 2, 2, slots, cw), BF16),
            pltpu.VMEM((CHUNKS, 2, 2, slots, cw), BF16),
            pltpu.VMEM((CHUNKS, 2, 2, slots, cw), BF16),
            pltpu.VMEM((CHUNKS, 2, slots, cw), BF16),
            pltpu.VMEM((CHUNKS, 2, slots, cw), BF16),
            pltpu.VMEM((CHUNKS, slots, cw), BF16),
            pltpu.VMEM((CHUNKS, groups, CAP, cw), BF16),
            dma((8 + CHUNKS,)),
            dma((groups + 1,)),
            dma((groups, 2)),
            dma((groups,)),
            dma((groups, 2)),
            dma((n_ctx, 2)),
            dma((CHUNKS, groups)),
            dma((CHUNKS, groups)),
            dma((7, CHUNKS)),
            dma((CHUNKS, SPLIT)),
            dma((3, CHUNKS)),
            dma((3, CHUNKS)),
            dma((CHUNKS, groups)),
            dma((CHUNKS, groups)),
        ],
        compiler_params=pltpu.CompilerParams(
            collective_id=0, has_side_effects=True, vmem_limit_bytes=67043328
        ),
    )(ids.T, gates.T, klat, krope, tok, qn, qr, ku, vu, gw, uw, dw)
    rout, att = pl.pallas_call(
        finish,
        grid=(CHUNKS,),
        out_shape=(jax.ShapeDtypeStruct(tok.shape, BF16), jax.ShapeDtypeStruct(att.shape, BF16)),
        in_specs=[
            pl.BlockSpec((1, groups, CAP, cw), lambda i: (i, 0, 0, 0)),
            pl.BlockSpec((tokens, lanes), lambda i: (0, 0)),
            pl.BlockSpec((rows, out_width // CHUNKS), lambda i: (0, i)),
        ],
        out_specs=(
            pl.BlockSpec((tokens, cw), lambda i: (0, i)),
            pl.BlockSpec((rows, out_width // CHUNKS), lambda i: (0, i)),
        ),
    )(res, wmix, att)
    return att, rout


def solution(mesh):
    body = functools.partial(local, mesh.shape["ctx"], mesh.shape["sec"])
    both = ("ctx", "sec")
    return jax.shard_map(
        body,
        mesh=mesh,
        in_specs=(
            P("ctx", "sec"),
            P("ctx", "sec"),
            P("ctx", None),
            P("ctx", None),
            P("sec", None, None),
            P("sec", None, None),
            P(both, None),
            P(both, None),
            P(both, None),
            P(None, both),
            P(None, both),
            P(both, None),
        ),
        out_specs=(P("ctx", "sec"), P(both, None)),
        check_vma=False,
    )
```

```python
import functools

import jax
import jax.numpy as jnp
from jax import lax
from jax.experimental import pallas as pl
from jax.experimental.pallas import tpu as pltpu
from jax.sharding import PartitionSpec as P

CAP = 4
SPLIT = 8
CHUNKS = 4
LOG2E = 1.4426950408889634
MESH_ID = pl.DeviceIdType.MESH
F32 = jnp.float32
BF16 = jnp.bfloat16
NT = (((1,), (1,)), ((), ()))


def kernel(
    dims,
    ids_ref,
    gates_ref,
    klat_ref,
    krope_ref,
    tok_hbm,
    qn_hbm,
    qr_hbm,
    ku_hbm,
    vu_hbm,
    gw_hbm,
    uw_hbm,
    dw_hbm,
    att_ref,
    resb,
    wmix,
    tok,
    qn,
    qr,
    ku,
    vu,
    gw,
    uw,
    dw,
    qcat,
    keys,
    outg,
    zbuf,
    arr,
    acc,
    part,
    r1,
    s1,
    r2,
    s2,
    r3,
    rbuf,
    load_sem,
    kz_send,
    kx_send,
    ky_send,
    kc_send,
    krecv,
    zsend,
    zrecv,
    asend,
    arecv,
    rsend,
    rrecv,
    bsend,
    brecv,
):
    groups, n_sec, rows, heads, lat, ropew, nope, hb = dims
    slots = groups * CAP
    width = tok.shape[1]
    cw = width // CHUNKS
    tokens = tok.shape[0]
    sent = lat + 2 * ropew
    ctx = lax.axis_index("ctx")
    sec = lax.axis_index("sec")
    me = ctx * n_sec + sec
    g = me // SPLIT
    m = lax.rem(me, SPLIT)
    bx = lax.rem(m, 2)
    bc = lax.rem(m // 2, 2)
    by = m // 4
    mx = m + 1 - 2 * bx
    mc = m + 2 - 4 * bc
    my = m + 4 - 8 * by
    mxy = mx + my - m

    def dev(group, member):
        index = group * SPLIT + member
        return (index // n_sec, lax.rem(index, n_sec))

    pending = []

    def rcopy(src, dst, ss, rs, target):
        return pltpu.make_async_remote_copy(
            src_ref=src, dst_ref=dst, send_sem=ss, recv_sem=rs,
            device_id=target, device_id_type=MESH_ID,
        )

    def send(src, dst, ss, rs, target):
        cp = rcopy(src, dst, ss, rs, target)
        cp.start()
        pending.append(cp)
        return cp

    nx, nc, ny = dev(g, mx), dev(g, mc), dev(g, my)
    others = [lax.rem(g + step, groups) for step in range(1, groups)]
    every = [g] + others

    tok_loads = []
    for c in range(CHUNKS):
        cols = pl.ds(c * cw, cw)
        tok_loads.append(
            pltpu.make_async_copy(tok_hbm.at[:, cols], tok.at[:, cols], load_sem.at[8 + c])
        )
        tok_loads[c].start()

    barrier = pltpu.get_barrier_semaphore()
    for target in [nx, nc, ny] + [dev(o, m) for o in others]:
        pl.semaphore_signal(barrier, inc=1, device_id=target, device_id_type=MESH_ID)

    pairs = [
        (qn_hbm, qn), (qr_hbm, qr), (ku_hbm, ku),
        (gw_hbm, gw), (uw_hbm, uw), (dw_hbm, dw), (vu_hbm, vu),
    ]
    loads = [None]
    for i, (a, b) in enumerate(pairs):
        loads.append(pltpu.make_async_copy(a, b, load_sem.at[i]))

    own_keys = keys.at[ctx]
    own_keys[:, :lat] = klat_ref[...]
    own_keys[:, lat:sent] = jnp.concatenate([krope_ref[...], krope_ref[...]], axis=1)

    pl.semaphore_wait(barrier, 3 + len(others))
    part_rows = rows // 2

    def kpiece(shard, which):
        return keys.at[shard, pl.ds(pl.multiple_of(which * part_rows, part_rows), part_rows), pl.ds(0, sent)]

    def kwhole(shard):
        return keys.at[shard, :, pl.ds(0, sent)]

    def kshard(group, member):
        return (group * SPLIT + member) // n_sec

    def ksend(group, member, which, sem, target):
        shard = kshard(group, member)
        piece = kpiece(shard, which)
        send(piece, piece, sem, krecv.at[shard, which], target)

    def karrive(group, member, which):
        shard = kshard(group, member)
        piece = kpiece(shard, which)
        rcopy(piece, piece, kz_send.at[0], krecv.at[shard, which], nx).wait_recv()

    for i, o in enumerate(others):
        ksend(g, m, bx, kz_send.at[i], dev(o, m))
    for which in range(2):
        ksend(g, m, which, kz_send.at[groups - 1 + which], ny)

    lanes = wmix.shape[1]
    row = lax.broadcasted_iota(jnp.int32, (lanes, tokens), 0)
    slot = row & (slots - 1)
    expert = slot // CAP
    matches = jnp.zeros((lanes, tokens), F32)
    gate = jnp.zeros((lanes, tokens), F32)
    for k in range(ids_ref.shape[0]):
        hit = ids_ref[k : k + 1, :] == expert
        matches = jnp.where(hit, 1.0, matches)
        gate = gate + jnp.where(hit, gates_ref[k : k + 1, :], 0.0)
    earlier = (
        lax.broadcasted_iota(jnp.int32, (tokens, tokens), 0)
        < lax.broadcasted_iota(jnp.int32, (tokens, tokens), 1)
    )
    rank = jnp.dot(
        matches.astype(BF16), jnp.where(earlier, 1.0, 0.0).astype(BF16), preferred_element_type=F32
    )
    chosen = jnp.where(rank == (slot & (CAP - 1)).astype(F32), matches, 0.0)
    picker = chosen[:slots].astype(BF16)

    for c in range(CHUNKS):
        tok_loads[c].wait()
        picked = jnp.dot(picker, tok[:, c * cw : (c + 1) * cw], preferred_element_type=F32)
        for e in range(groups):
            outg[c, e] = picked[e * CAP : (e + 1) * CAP].astype(BF16)
        for i, o in enumerate(others):
            send(outg.at[c, o], zbuf.at[c, g], zsend.at[c, i], zrecv.at[c, g], dev(o, m))

    for load in loads[1:4]:
        load.start()
    weight = chosen * gate
    w1 = weight.astype(BF16).astype(F32)
    w2 = (weight - w1).astype(BF16).astype(F32)
    w3 = weight - w1 - w2
    wmix[...] = jnp.where(
        row < slots, w1, jnp.where(row < 2 * slots, w2, jnp.where(row < 3 * slots, w3, 0.0))
    ).T.astype(BF16)

    maskw = keys.shape[2] - sent

    @pl.loop(0, keys.shape[0])
    def _(shard):
        key_place = shard * rows + lax.broadcasted_iota(jnp.int32, (rows, maskw), 0)
        query = lax.broadcasted_iota(jnp.int32, (rows, maskw), 1)
        hidden_key = (key_place > ctx * rows + query) & (query < rows)
        keys[shard, :, sent:] = jnp.where(hidden_key, -1e30, 0.0).astype(BF16)

    loads[1].wait()
    loads[2].wait()
    loads[3].wait()
    for load in loads[4:]:
        load.start()
    unit = jnp.where(
        lax.broadcasted_iota(jnp.int32, (rows, maskw), 0)
        == lax.broadcasted_iota(jnp.int32, (rows, maskw), 1),
        1.0,
        0.0,
    ).astype(BF16)

    def query_latents(first, last):
        @pl.loop(first, last)
        def _(p):
            rope = qr[:, pl.ds(pl.multiple_of(p * 2 * ropew, 2 * ropew), 2 * ropew)]
            low = lax.broadcasted_iota(jnp.int32, rope.shape, 1) < ropew
            for k in range(2):
                h = p * 2 + k
                q = qn[:, pl.ds(pl.multiple_of(h * nope, nope), nope)]
                latent = lax.dot_general(q, ku[h], NT, preferred_element_type=F32)
                place = pl.ds(pl.multiple_of(h * rows, rows), rows)
                qcat[place, :lat] = latent.astype(BF16)
                keep = low if k == 0 else jnp.logical_not(low)
                qcat[place, lat:sent] = jnp.where(keep, rope.astype(F32), 0.0).astype(BF16)
                qcat[place, sent:] = unit

    half_pairs = heads // 4
    query_latents(0, half_pairs)

    for i, o in enumerate(others):
        karrive(o, m, bx)
        ksend(o, m, bx, kx_send.at[i, 0], nx)
        ksend(o, m, bx, ky_send.at[i], ny)

    def spread(kind, member, c, target):
        piece = arr.at[c, member]
        send(piece, piece, asend.at[kind, c], arecv.at[c, member], target)

    def arrive(member, c):
        piece = arr.at[c, member]
        rcopy(piece, piece, asend.at[0, c], arecv.at[c, member], nx).wait_recv()

    def start_chunk(c):
        for i, o in enumerate(others):
            rcopy(outg.at[c, o], zbuf.at[c, o], zsend.at[c, i], zrecv.at[c, o], dev(o, m)).wait_recv()
        zbuf[c, g] = outg[c, g]
        blocks = [zbuf[c, e].astype(F32) for e in range(groups)]
        arr[c, m] = jnp.concatenate(blocks, axis=0).astype(BF16)
        spread(0, m, c, nx)
        spread(1, m, c, ny)
        spread(2, m, c, nc)

    def forward_chunk(c):
        arrive(mx, c)
        if c % 2 == 0:
            spread(3, mx, c, ny)
        spread(4, mx, c, nc)
        arrive(my, c)
        if c % 2 == 1:
            spread(3, my, c, nx)
        spread(5, my, c, nc)

    count = SPLIT * slots

    def finish_chunk(c):
        arrive(mxy, c)
        spread(6, mxy, c, nc)

    def gate_up(c):
        for member in (mc, mx + mc - m, my + mc - m, mxy + mc - m):
            arrive(member, c)
        x = arr[c].reshape(count, cw)
        g_part = jnp.dot(x, gw[c * cw : (c + 1) * cw], preferred_element_type=F32)
        u_part = jnp.dot(x, uw[c * cw : (c + 1) * cw], preferred_element_type=F32)
        if c == 0:
            acc[0] = g_part
            acc[1] = u_part
        else:
            acc[0] += g_part
            acc[1] += u_part

    start_chunk(0)
    start_chunk(1)
    for i, o in enumerate(others):
        karrive(o, my, bx)
        ksend(o, my, bx, kx_send.at[i, 1], nx)
    forward_chunk(0)
    start_chunk(2)
    forward_chunk(1)
    start_chunk(3)
    finish_chunk(0)
    forward_chunk(2)
    finish_chunk(1)
    forward_chunk(3)

    shard = kshard(g, m)
    send(kwhole(shard), kwhole(shard), kc_send.at[0, 0], krecv.at[shard, 0], nc)
    for i, o in enumerate(others):
        karrive(o, m, 1 - bx)
        shard = kshard(o, m)
        send(kwhole(shard), kwhole(shard), kc_send.at[i + 1, 0], krecv.at[shard, 0], nc)
    for i, o in enumerate(every):
        karrive(o, my, 1 - bx)
        if i == 0:
            karrive(o, my, bx)
        shard = kshard(o, my)
        send(kwhole(shard), kwhole(shard), kc_send.at[i, 1], krecv.at[shard, 0], nc)

    loads[4].wait()
    loads[5].wait()
    gate_up(0)
    finish_chunk(2)
    gate_up(1)
    finish_chunk(3)
    query_latents(half_pairs, heads // 2)
    gate_up(2)
    gate_up(3)
    gate_act = acc[0]
    hidden = (gate_act / (1.0 + jnp.exp(-gate_act)) * acc[1]).astype(BF16)

    c1, c2, c3 = [], [], []
    loads[6].wait()

    def down(c):
        value = jnp.dot(hidden, dw[:, c * cw : (c + 1) * cw], preferred_element_type=F32)
        part[c] = value.astype(BF16).reshape(2, 2, 2, slots, cw)
        c1.append(send(part.at[c, :, 1 - bc], r1.at[c], rsend.at[0, c], rrecv.at[0, c], nc))

    def sum_cores(c):
        c1[c].wait_recv()
        for a in range(2):
            for b in range(2):
                s1[c, a, b] = (part[c, a, bc, b].astype(F32) + r1[c, a, b].astype(F32)).astype(BF16)
        src = s1.at[c, :, 1 - bx] if c % 2 == 0 else s1.at[c, 1 - by]
        c2.append(send(src, r2.at[c], rsend.at[1, c], rrecv.at[1, c], nx if c % 2 == 0 else ny))

    def sum_first(c):
        c2[c].wait_recv()
        for a in range(2):
            mine = s1[c, a, bx] if c % 2 == 0 else s1[c, by, a]
            s2[c, a] = (mine.astype(F32) + r2[c, a].astype(F32)).astype(BF16)
        keep = by if c % 2 == 0 else bx
        c3.append(send(s2.at[c, 1 - keep], r3.at[c], rsend.at[2, c], rrecv.at[2, c],
                       ny if c % 2 == 0 else nx))

    def sum_second(c):
        c3[c].wait_recv()
        keep = by if c % 2 == 0 else bx
        total = s2[c, keep].astype(F32) + r3[c].astype(F32)
        for e in range(groups):
            rbuf[c, e] = total[e * CAP : (e + 1) * CAP].astype(BF16)
        for i, o in enumerate(others):
            send(rbuf.at[c, o], resb.at[c, g], bsend.at[c, i], brecv.at[c, g], dev(o, m))
        resb[c, g] = rbuf[c, g]

    for c in range(CHUNKS):
        down(c)

    loads[7].wait()
    for o in every:
        for member in (mc, my + mc - m):
            shard = kshard(o, member)
            rcopy(kwhole(shard), kwhole(shard), kc_send.at[0, 0], krecv.at[shard, 0], nc).wait_recv()

    seq = keys.shape[0] * keys.shape[1]
    block = hb * rows
    scale = (nope + ropew) ** -0.5 * LOG2E

    def attend(first, last):
        @pl.loop(first, last)
        def _(b):
            q = qcat[pl.ds(pl.multiple_of(b * block, block), block)]
            kk = keys[...].reshape(seq, keys.shape[2])
            score = lax.dot_general(q, kk, NT, preferred_element_type=F32)
            top = jnp.max(score, axis=1, keepdims=True)
            expo = jnp.exp2((score - top) * scale)
            total = jnp.sum(expo, axis=1, keepdims=True)
            mixed = jnp.dot(expo.astype(BF16), kk[:, :lat], preferred_element_type=F32)
            mixed = (mixed / total).astype(BF16)
            for k in range(hb):
                h = b * hb + k
                value = jnp.dot(
                    mixed[k * rows : (k + 1) * rows], vu[h], preferred_element_type=F32
                )
                vdim = value.shape[1]
                att_ref[:, pl.ds(pl.multiple_of(h * vdim, vdim), vdim)] = value.astype(BF16)

    nb = heads // hb
    eighth = nb // 8
    attend(0, eighth)
    for c in range(CHUNKS):
        sum_cores(c)
    attend(eighth, 3 * eighth)
    for c in range(CHUNKS):
        sum_first(c)
    attend(3 * eighth, 5 * eighth)
    for c in range(CHUNKS):
        sum_second(c)
    attend(5 * eighth, nb)

    for c in range(CHUNKS):
        for i, o in enumerate(others):
            rcopy(rbuf.at[c, o], resb.at[c, o], bsend.at[c, i], brecv.at[c, o], dev(o, m)).wait_recv()
    for cp in pending:
        cp.wait_send()


def finish(res_ref, wmix_ref, att_in, rout_ref, att_out):
    chunks, groups, _, cw = res_ref.shape
    att_out[...] = att_in[...]
    for c in range(chunks):
        blocks = [res_ref[c, e].astype(F32) for e in range(groups)]
        block_rows = jnp.concatenate(blocks, axis=0).astype(BF16)
        tall = jnp.concatenate([block_rows] * 3, axis=0)
        rout_ref[:, c * cw : (c + 1) * cw] = jnp.dot(
            wmix_ref[:, : tall.shape[0]], tall, preferred_element_type=F32
        ).astype(BF16)


def local(n_ctx, n_sec, qn, qr, klat, krope, ku, vu, tok, ids, gates, gw, uw, dw):
    devices = n_ctx * n_sec
    groups = devices // SPLIT
    slots = groups * CAP
    rows = qn.shape[0]
    heads, lat, nope = ku.shape
    ropew = krope.shape[1]
    tokens, width = tok.shape
    cw = width // CHUNKS
    kw = lat + 2 * ropew + 128
    hb = 4 if n_ctx * rows <= 2048 else 1
    lanes = -(-3 * slots // 128) * 128
    dims = (groups, n_sec, rows, heads, lat, ropew, nope, hb)
    v = pl.BlockSpec(memory_space=pltpu.VMEM)
    a = pl.BlockSpec(memory_space=pl.ANY)
    dma = pltpu.SemaphoreType.DMA
    out_width = heads * vu.shape[2]
    att, res, wmix = pl.pallas_call(
        functools.partial(kernel, dims),
        out_shape=(
            jax.ShapeDtypeStruct((rows, out_width), BF16),
            jax.ShapeDtypeStruct((CHUNKS, groups, CAP, cw), BF16),
            jax.ShapeDtypeStruct((tokens, lanes), BF16),
        ),
        in_specs=[v, v, v, v] + [a] * 8,
        out_specs=(v, v, v),
        scratch_shapes=[
            pltpu.VMEM(tok.shape, BF16),
            pltpu.VMEM(qn.shape, BF16),
            pltpu.VMEM(qr.shape, BF16),
            pltpu.VMEM(ku.shape, BF16),
            pltpu.VMEM(vu.shape, BF16),
            pltpu.VMEM(gw.shape, BF16),
            pltpu.VMEM(uw.shape, BF16),
            pltpu.VMEM(dw.shape, BF16),
            pltpu.VMEM((heads * rows, kw), BF16),
            pltpu.VMEM((n_ctx, rows, kw), BF16),
            pltpu.VMEM((CHUNKS, groups, CAP, cw), BF16),
            pltpu.VMEM((CHUNKS, groups, CAP, cw), BF16),
            pltpu.VMEM((CHUNKS, SPLIT, slots, cw), BF16),
            pltpu.VMEM((2, SPLIT * slots, gw.shape[1]), F32),
            pltpu.VMEM((CHUNKS, 2, 2, 2, slots, cw), BF16),
            pltpu.VMEM((CHUNKS, 2, 2, slots, cw), BF16),
            pltpu.VMEM((CHUNKS, 2, 2, slots, cw), BF16),
            pltpu.VMEM((CHUNKS, 2, slots, cw), BF16),
            pltpu.VMEM((CHUNKS, 2, slots, cw), BF16),
            pltpu.VMEM((CHUNKS, slots, cw), BF16),
            pltpu.VMEM((CHUNKS, groups, CAP, cw), BF16),
            dma((8 + CHUNKS,)),
            dma((groups + 1,)),
            dma((groups, 2)),
            dma((groups,)),
            dma((groups, 2)),
            dma((n_ctx, 2)),
            dma((CHUNKS, groups)),
            dma((CHUNKS, groups)),
            dma((7, CHUNKS)),
            dma((CHUNKS, SPLIT)),
            dma((3, CHUNKS)),
            dma((3, CHUNKS)),
            dma((CHUNKS, groups)),
            dma((CHUNKS, groups)),
        ],
        compiler_params=pltpu.CompilerParams(
            collective_id=0, has_side_effects=True, vmem_limit_bytes=67043328
        ),
    )(ids.T, gates.T, klat, krope, tok, qn, qr, ku, vu, gw, uw, dw)
    rout, att = pl.pallas_call(
        finish,
        out_shape=(jax.ShapeDtypeStruct(tok.shape, BF16), jax.ShapeDtypeStruct(att.shape, BF16)),
        in_specs=[v, v, v],
        out_specs=(v, v),
    )(res, wmix, att)
    return att, rout


def solution(mesh):
    body = functools.partial(local, mesh.shape["ctx"], mesh.shape["sec"])
    both = ("ctx", "sec")
    return jax.shard_map(
        body,
        mesh=mesh,
        in_specs=(
            P("ctx", "sec"),
            P("ctx", "sec"),
            P("ctx", None),
            P("ctx", None),
            P("sec", None, None),
            P("sec", None, None),
            P(both, None),
            P(both, None),
            P(both, None),
            P(None, both),
            P(None, both),
            P(both, None),
        ),
        out_specs=(P("ctx", "sec"), P(both, None)),
        check_vma=False,
    )
```
